256 devices in a mesh: hi: 8 (over y, core), lo: 32 (over x, z).
Axes of the slice: x: 4, y: 4, z: 8, core: 2. Of those that a mesh axis runs over, the one named last changes fastest.
Arguments:
- vectors: bfloat16 [128, 524288], P(None, ('hi', 'lo')), may hold values from -6 to 6
- leaves: bfloat16 [524288, 512], P(('hi', 'lo')), may hold values from -0.25 to 0.25
- u_local: bfloat16 [2, 524288, 128], P(None, ('hi', 'lo')), may hold values from -0.5 to 0.5
- v_local: bfloat16 [2, 524288, 128], P(None, ('hi', 'lo')), may hold values from -6 to 6
- u_upper: bfloat16 [8, 524288, 128], P(None, ('hi', 'lo')), may hold values from -0.5 to 0.5
- v_upper: bfloat16 [8, 524288, 128], P(None, ('hi', 'lo')), may hold values from -6 to 6
Outputs:
- krylov_last: bfloat16 [128, 524288], P(None, ('hi', 'lo'))
The draws below stay inside these ranges and needn't reach their ends.
All inputs are finite; a program needn't handle non-finite values.
Results may differ from the reference program's by a relative error of at most 0.018.
Values sent between devices are 32-bit elements; how exact they have to be, the bound alone decides.
No kernel may reach another device: no remote copies, remote signals or barrier semaphores. Data moves between devices by JAX's collectives and lax.ppermute only.
A program may use at most 64 MiB of HBM per device.

```python
import math
import jax
import jax.numpy as jnp

LEAF = 512
RANK = 128
RHS = 128
LOCAL_LEVELS = 2
ITERS = 4
DIST_LEVELS = 8
NROWS = 524288


def shard_levels(stream_key, dims, shards, low, top_value):
    def one(axis_at, shards_of):
        steps = jax.random.uniform(jax.random.fold_in(jax.random.fold_in(stream_key, 6), axis_at), (shards_of,), jnp.float32, low / len(shards), top_value / len(shards))
        return jnp.repeat(jnp.exp(steps), dims[axis_at] // shards_of).reshape((-1,) + (1,) * (len(dims) - axis_at - 1))

    gain = one(*shards[0])
    for cut in shards[1:]:
        gain = gain * one(*cut)
    return gain


def centred(own_key, shape, spread, reach, cuts=(), kind=jnp.bfloat16):
    values = spread * jax.random.normal(own_key, shape, jnp.float32)
    if cuts:
        values = values * shard_levels(own_key, shape, cuts, -0.22, 0.18)
    return jnp.clip(values, -reach, reach).astype(kind)


def setup_inputs(seed: int = 0) -> dict:
    splits = jax.random.split(jax.random.key(seed), 7)
    vectors = centred(splits[0], (RHS, NROWS), 1.0, 6.0, ((1, 256),))
    leaves = centred(splits[1], (NROWS, LEAF), LEAF ** -0.5, 0.25, ((0, 256),))
    u_local = centred(splits[2], (LOCAL_LEVELS, NROWS, RANK), RANK ** -0.5, 0.5, ((1, 256),))
    v_local = centred(splits[3], (LOCAL_LEVELS, NROWS, RANK), 1.0, 6.0, ((1, 256),))
    u_upper = centred(splits[4], (DIST_LEVELS, NROWS, RANK), RANK ** -0.5, 0.5, ((1, 256),))
    v_upper = centred(splits[5], (DIST_LEVELS, NROWS, RANK), 1.0, 6.0, ((1, 256),))
    return {"vectors": vectors, "leaves": leaves, "u_local": u_local, "v_local": v_local, "u_upper": u_upper, "v_upper": v_upper}


def level_factors(level, u_local, v_local, u_upper, v_upper):
    if level < LOCAL_LEVELS:
        return (u_local[level], v_local[level])
    return (u_upper[level - LOCAL_LEVELS], v_upper[level - LOCAL_LEVELS])

def apply_operator(state, leaves, u_local, v_local, u_upper, v_upper):
    total_rows = state.shape[1]
    wide = state.shape[0]
    state_f = state.astype(jnp.float32)
    blocks = leaves.reshape(total_rows // LEAF, LEAF, LEAF).astype(jnp.float32)
    result = jnp.einsum('gij,cgj->cgi', blocks, state_f.reshape(wide, total_rows // LEAF, LEAF))
    result = result.reshape(wide, total_rows)
    level_count = LOCAL_LEVELS + DIST_LEVELS
    for level in range(level_count):
        u_mat, v_mat = level_factors(level, u_local, v_local, u_upper, v_upper)
        node_rows = LEAF * 2 ** level
        groups = total_rows // node_rows
        coef = jnp.einsum('gsr,cgs->gcr', v_mat.astype(jnp.float32).reshape(groups, node_rows, RANK), state_f.reshape(wide, groups, node_rows))
        coef = coef.reshape(groups // 2, 2, wide, RANK)[:, ::-1].reshape(groups, wide, RANK)
        coef = (coef * (1.0 / math.sqrt(node_rows * level_count))).astype(jnp.bfloat16)
        added = jnp.einsum('gsr,gcr->cgs', u_mat.astype(jnp.float32).reshape(groups, node_rows, RANK), coef.astype(jnp.float32))
        result = result + added.reshape(wide, total_rows)
    return result.astype(jnp.bfloat16)

def reference(vectors, leaves, u_local, v_local, u_upper, v_upper):
    state = vectors
    for step in range(ITERS):
        state = apply_operator(state, leaves, u_local, v_local, u_upper, v_upper)
    return state
```

```python
import math

import jax
import jax.numpy as jnp
from jax import lax
from jax.sharding import PartitionSpec as P

ITERS = 4
AXES = ("hi", "lo")


def sibling_sums(parts):
    levels, wide, rank_cols = parts.shape
    count = lax.axis_size("hi") * lax.axis_size("lo")
    slice_rows = levels * wide // count
    gathered = lax.all_to_all(parts.reshape(count, slice_rows, rank_cols), AXES, 0, 0)
    me = lax.axis_index("hi") * lax.axis_size("lo") + lax.axis_index("lo")
    level = me * slice_rows // wide
    rows = lax.broadcasted_iota(jnp.int32, (count, count), 0)
    cols = lax.broadcasted_iota(jnp.int32, (count, count), 1)
    sibling = (lax.shift_right_logical(rows ^ cols, level) == 1).astype(jnp.float32)
    sums = jnp.einsum("ds,sir->dir", sibling, gathered, precision=lax.Precision.HIGHEST)
    return lax.all_to_all(sums, AXES, 0, 0).reshape(levels, wide, rank_cols)


def apply_operator(state, leaves, u_local, v_local, u_upper, v_upper):
    wide, dev_rows = state.shape
    leaf_rows = leaves.shape[1]
    local_count = u_local.shape[0]
    upper_count = u_upper.shape[0]
    level_count = local_count + upper_count
    rank_cols = u_local.shape[2]
    parts = jnp.einsum("bsr,cs->bcr", v_upper, state, preferred_element_type=jnp.float32)
    found = sibling_sums(parts)
    blocks = leaves.reshape(dev_rows // leaf_rows, leaf_rows, leaf_rows)
    result = jnp.einsum(
        "gij,cgj->cgi",
        blocks,
        state.reshape(wide, dev_rows // leaf_rows, leaf_rows),
        preferred_element_type=jnp.float32,
    ).reshape(wide, dev_rows)
    for level in range(local_count):
        node_rows = leaf_rows * 2**level
        groups = dev_rows // node_rows
        coef = jnp.einsum(
            "gsr,cgs->gcr",
            v_local[level].reshape(groups, node_rows, rank_cols),
            state.reshape(wide, groups, node_rows),
            preferred_element_type=jnp.float32,
        )
        coef = coef.reshape(groups // 2, 2, wide, rank_cols)[:, ::-1].reshape(
            groups, wide, rank_cols
        )
        coef = (coef * (1.0 / math.sqrt(node_rows * level_count))).astype(jnp.bfloat16)
        added = jnp.einsum(
            "gsr,gcr->cgs",
            u_local[level].reshape(groups, node_rows, rank_cols),
            coef,
            preferred_element_type=jnp.float32,
        )
        result = result + added.reshape(wide, dev_rows)
    factors = jnp.array(
        [
            1.0 / math.sqrt(dev_rows * 2**level_bit * level_count)
            for level_bit in range(upper_count)
        ],
        dtype=jnp.float32,
    )
    coefs = (found * factors[:, None, None]).astype(jnp.bfloat16)
    result = result + jnp.einsum("bsr,bcr->cs", u_upper, coefs, preferred_element_type=jnp.float32)
    return result.astype(jnp.bfloat16)


def local(vectors, leaves, u_local, v_local, u_upper, v_upper):
    state = vectors
    for step in range(ITERS):
        state = apply_operator(state, leaves, u_local, v_local, u_upper, v_upper)
    return state


def solution(mesh):
    return jax.shard_map(
        local,
        mesh=mesh,
        in_specs=(
            P(None, ("hi", "lo")),
            P(("hi", "lo"), None),
            P(None, ("hi", "lo"), None),
            P(None, ("hi", "lo"), None),
            P(None, ("hi", "lo"), None),
            P(None, ("hi", "lo"), None),
        ),
        out_specs=P(None, ("hi", "lo")),
        check_vma=False,
    )
```

```python
import functools
import math

import jax
import jax.numpy as jnp
from jax import lax
from jax.experimental import pallas as pl
from jax.experimental.pallas import tpu as pltpu
from jax.sharding import PartitionSpec as P

ITERS = 4
BLOCKS = 2
TILE = 512
NT = (((1,), (1,)), ((), ()))
VMEM = pl.BlockSpec(memory_space=pltpu.VMEM)


def dot(a, b):
    return jnp.dot(a, b, preferred_element_type=jnp.float32)


def dot_nt(a, b):
    return lax.dot_general(a, b, NT, preferred_element_type=jnp.float32)


def which_half():
    return lax.axis_index("lo") % 2 == 1


def which_quarter():
    lo = lax.axis_index("lo")
    return (lax.div(lo, 2) + lax.div(lo, 4)) % 2 == 1


def split(second, value, send_ref, send_at, keep_ref, keep_at):
    half = value.shape[0] // 2
    low, high = value[:half], value[half:]
    send_ref[pl.ds(send_at, half), :] = jnp.where(second, low, high)
    keep_ref[pl.ds(keep_at, half), :] = jnp.where(second, high, low)


def merge(second, mine, theirs):
    return jnp.concatenate([jnp.where(second, theirs, mine), jnp.where(second, mine, theirs)], axis=0)


def project(state, v_ref, outs):
    odd = which_half()
    wide = state.shape[0] * 2 // len(outs)
    half = wide // 2
    rank = v_ref.shape[2]
    for level in range(0, v_ref.shape[0], 2):
        both = dot(state, jnp.concatenate([v_ref[level], v_ref[level + 1]], axis=1))
        for one, part in ((level, both[:, :rank]), (level + 1, both[:, rank:])):
            for block in range(len(outs) // 2):
                send_ref, keep_ref = outs[2 * block : 2 * block + 2]
                rows = part[block * wide : (block + 1) * wide]
                if one == 0:
                    send_ref[pl.ds(0, wide), :] = rows
                else:
                    split(odd, rows, send_ref, wide + (one - 1) * half, keep_ref, (one - 1) * half)


def first_kernel(state_ref, v_ref, *outs):
    project(state_ref[...], v_ref, outs)


def expand(scales, found, base_ref, u_ref, state_ref):
    odd = which_half()
    blocks = []
    for block in range(0, len(found), 3):
        first_ref, own_ref, other_ref = found[block : block + 3]
        half = own_ref.shape[0] // (u_ref.shape[0] - 1)
        coefs = [first_ref[pl.ds(0, 2 * half), :]]
        for i in range(u_ref.shape[0] - 1):
            rows = pl.ds(i * half, half)
            coefs.append(merge(odd, own_ref[rows, :], other_ref[rows, :]))
        blocks.append(
            jnp.concatenate([(coef * scale).astype(jnp.bfloat16) for coef, scale in zip(coefs, scales)], axis=1)
        )
    coefs = jnp.concatenate(blocks, axis=0)
    for start in range(0, state_ref.shape[1], TILE):
        rows = pl.ds(start, TILE)
        bases = jnp.concatenate([u_ref[i, rows, :] for i in range(u_ref.shape[0])], axis=1)
        state_ref[:, rows] = (base_ref[:, rows] + dot_nt(coefs, bases)).astype(jnp.bfloat16)


def middle_kernel(scales, *refs):
    found, (base_ref, u_ref, v_ref, state_ref), outs = refs[: 3 * BLOCKS], refs[3 * BLOCKS : 3 * BLOCKS + 4], refs[3 * BLOCKS + 4 :]
    expand(scales, found, base_ref, u_ref, state_ref)
    project(state_ref[...], v_ref, outs)


def last_kernel(scales, *refs):
    *found, base_ref, u_ref, state_ref = refs
    expand(scales, found, base_ref, u_ref, state_ref)


def local_kernel(scales, state_ref, leaves_ref, u_ref, v_ref, base_ref):
    dev_rows, leaf = leaves_ref.shape
    levels = u_ref.shape[0]
    coefs = []
    for level in range(levels):
        size = leaf * 2**level
        coefs.append(
            [
                (
                    dot(state_ref[:, pl.ds(start, size)], v_ref[level, pl.ds(start, size), :])
                    * scales[level]
                ).astype(jnp.bfloat16)
                for start in range(0, dev_rows, size)
            ]
        )
    for index, start in enumerate(range(0, dev_rows, leaf)):
        rows = pl.ds(start, leaf)
        left = [state_ref[:, rows]]
        right = [leaves_ref[rows, :]]
        for level in range(levels):
            left.append(coefs[level][(index >> level) ^ 1])
            right.append(u_ref[level, rows, :])
        base_ref[:, rows] = dot_nt(jnp.concatenate(left, axis=1), jnp.concatenate(right, axis=1))


def quarter_kernel(arrived_ref, kept_ref, send_ref, keep_ref):
    second = which_quarter()
    skip = arrived_ref.shape[0] - kept_ref.shape[0]
    half = skip // 2
    for i in range(kept_ref.shape[0] // half):
        total = kept_ref[pl.ds(i * half, half), :] + arrived_ref[pl.ds(skip + i * half, half), :]
        if i == 0:
            send_ref[pl.ds(0, half), :] = total
        else:
            split(second, total, send_ref, half + (i - 1) * half // 2, keep_ref, (i - 1) * half // 2)


def add_kernel(arrived_ref, kept_ref, out_ref):
    rows = out_ref.shape[0]
    out_ref[...] = (
        kept_ref[pl.ds(kept_ref.shape[0] - rows, rows), :]
        + arrived_ref[pl.ds(arrived_ref.shape[0] - rows, rows), :]
    )


def join_kernel(*refs):
    *pieces, out_ref = refs
    rows = pieces[-1].shape[0]
    for i, ref in enumerate(pieces):
        out_ref[pl.ds(i * rows, rows), :] = ref[pl.ds(0, rows), :]


def halves_kernel(one_ref, own_ref, other_ref, out_ref):
    second = which_quarter()
    half = one_ref.shape[0] - own_ref.shape[0]
    out_ref[pl.ds(0, half), :] = one_ref[pl.ds(0, half), :]
    quarter = half // 2
    for i in range(own_ref.shape[0] // quarter):
        rows = pl.ds(i * quarter, quarter)
        out_ref[pl.ds((i + 1) * half, half), :] = merge(second, own_ref[rows, :], other_ref[rows, :])


def call(kernel, name, outs, *args):
    return pl.pallas_call(
        kernel,
        out_shape=outs,
        in_specs=[VMEM] * len(args),
        out_specs=jax.tree.map(lambda _: VMEM, outs),
        compiler_params=pltpu.CompilerParams(vmem_limit_bytes=6 * 2**20),
        name=name,
    )(*args)


def stack(rows, rank):
    return jax.ShapeDtypeStruct((rows, rank), jnp.float32)


def from_partner(value, axis, mask):
    pairs = [(source, source ^ mask) for source in range(lax.axis_size(axis))]
    return lax.ppermute(value, axis, pairs)


def exchange(send, keep):
    rank = send.shape[1]
    half = (send.shape[0] - keep.shape[0]) // 2
    quarter = half // 2
    upper = keep.shape[0] // half
    first = from_partner(send, "lo", 1)
    quarters = (upper - 1) * quarter
    send, keep = call(
        quarter_kernel, "quarter", (stack(half + quarters, rank), stack(quarters, rank)), first, keep
    )
    second = from_partner(send, "lo", 2)
    total = call(add_kernel, "add", stack(quarters, rank), second, keep)
    found = []
    for axis, mask in (("lo", 6), ("lo", 8), ("lo", 24), ("hi", 1), ("hi", 2), ("hi", 6)):
        arrived = from_partner(total, axis, mask)
        found.append(arrived)
        rows = total.shape[0] - quarter
        if rows:
            total = call(add_kernel, "add", stack(rows, rank), arrived, total)
    own = call(join_kernel, "join", stack(quarters, rank), *found)
    other = from_partner(own, "lo", 2)
    own = call(halves_kernel, "halves", stack(upper * half, rank), second, own, other)
    return first, own, from_partner(own, "lo", 1)


def local(vectors, leaves, u_local, v_local, u_upper, v_upper):
    wide, dev_rows = vectors.shape
    leaf = leaves.shape[1]
    rank = u_local.shape[2]
    local_count = u_local.shape[0]
    upper_count = u_upper.shape[0]
    level_count = local_count + upper_count
    scales = [1.0 / math.sqrt(leaf * 2**level * level_count) for level in range(level_count)]
    upper_scales = scales[local_count:]
    block = wide // BLOCKS
    half = block // 2
    part_shapes = (stack(block + (upper_count - 1) * half, rank), stack((upper_count - 1) * half, rank)) * BLOCKS
    state_shape = jax.ShapeDtypeStruct((wide, dev_rows), jnp.bfloat16)
    base_shape = jax.ShapeDtypeStruct((wide, dev_rows), jnp.float32)
    state = vectors
    parts = call(first_kernel, "first", part_shapes, state, v_upper)
    for step in range(ITERS):
        found = []
        for send, keep in zip(parts[::2], parts[1::2]):
            found += exchange(send, keep)
        base = call(
            functools.partial(local_kernel, scales[:local_count]), "local", base_shape, state, leaves, u_local, v_local
        )
        if step < ITERS - 1:
            state, *parts = call(
                functools.partial(middle_kernel, upper_scales), "middle", (state_shape, *part_shapes),
                *found, base, u_upper, v_upper,
            )
        else:
            state = call(functools.partial(last_kernel, upper_scales), "last", state_shape, *found, base, u_upper)
    return state


def solution(mesh):
    return jax.shard_map(
        local,
        mesh=mesh,
        in_specs=(
            P(None, ("hi", "lo")),
            P(("hi", "lo"), None),
            P(None, ("hi", "lo"), None),
            P(None, ("hi", "lo"), None),
            P(None, ("hi", "lo"), None),
            P(None, ("hi", "lo"), None),
        ),
        out_specs=P(None, ("hi", "lo")),
        check_vma=False,
    )
```

```python
import functools
import math

import jax
import jax.numpy as jnp
from jax import lax
from jax.experimental import pallas as pl
from jax.experimental.pallas import tpu as pltpu
from jax.sharding import PartitionSpec as P

ITERS = 4
TILE = 512
NT = (((1,), (1,)), ((), ()))
VMEM = pl.BlockSpec(memory_space=pltpu.VMEM)


def dot(a, b):
    return jnp.dot(a, b, preferred_element_type=jnp.float32)


def dot_nt(a, b):
    return lax.dot_general(a, b, NT, preferred_element_type=jnp.float32)


def position():
    lo = lax.axis_index("lo")
    return lo % 2 == 1, (lax.div(lo, 2) + lax.div(lo, 4)) % 2 == 1


def pick(one, two, pieces):
    return jnp.where(one, jnp.where(two, pieces[3], pieces[2]), jnp.where(two, pieces[1], pieces[0]))


def merge(second, mine, theirs):
    return jnp.concatenate([jnp.where(second, theirs, mine), jnp.where(second, mine, theirs)], axis=0)


def gather_quarters(own, near, next_, far):
    one, two = position()
    low = [jnp.where(one, near, own), jnp.where(one, far, next_)]
    high = [jnp.where(one, own, near), jnp.where(one, next_, far)]
    return jnp.concatenate([merge(two, *low), merge(two, *high)], axis=0)


def project(state, v_ref, outs):
    sends, keep_ref, early, early_keep_ref = outs[:3], outs[3], outs[4:7], outs[7]
    one, two = position()
    wide = state.shape[0]
    half, quarter = wide // 2, wide // 4
    rank = v_ref.shape[2]
    for level in range(0, v_ref.shape[0], 2):
        both = dot(state, jnp.concatenate([v_ref[level], v_ref[level + 1]], axis=1))
        for this, part in ((level, both[:, :rank]), (level + 1, both[:, rank:])):
            if this == 0:
                early[0][pl.ds(0, wide), :] = part
            elif this == 1:
                low, high = part[:half], part[half:]
                early[1][pl.ds(0, half), :] = jnp.where(one, high, low)
                early[2][pl.ds(0, half), :] = jnp.where(one, low, high)
            else:
                pieces = [part[i * quarter : (i + 1) * quarter] for i in range(4)]
                if this == 2:
                    targets = [(early[0], wide), (early[1], half), (early[2], half), (early_keep_ref, 0)]
                else:
                    start = (this - 3) * quarter
                    targets = [(ref, start) for ref in (*sends, keep_ref)]
                orders = ((2, 3, 0, 1), (1, 0, 3, 2), (3, 2, 1, 0), (0, 1, 2, 3))
                for (ref, start), order in zip(targets, orders):
                    ref[pl.ds(start, quarter), :] = pick(one, two, [pieces[i] for i in order])


def first_kernel(state_ref, v_ref, *outs):
    project(state_ref[...], v_ref, outs)


def expand(scales, zero_ref, own_ref, near_ref, next_ref, far_ref, base_ref, u_ref, state_ref):
    wide = base_ref.shape[0]
    half, quarter = wide // 2, wide // 4
    one, _ = position()
    coefs = [
        zero_ref[pl.ds(0, wide), :],
        merge(one, own_ref[pl.ds(0, half), :], near_ref[pl.ds(0, half), :]),
    ]
    for i in range(u_ref.shape[0] - 2):
        long, short = pl.ds(half + i * quarter, quarter), pl.ds(i * quarter, quarter)
        coefs.append(gather_quarters(own_ref[long, :], near_ref[long, :], next_ref[short, :], far_ref[short, :]))
    coefs = jnp.concatenate(
        [(coef * scale).astype(jnp.bfloat16) for coef, scale in zip(coefs, scales)], axis=1
    )
    for start in range(0, state_ref.shape[1], TILE):
        rows = pl.ds(start, TILE)
        bases = jnp.concatenate([u_ref[i, rows, :] for i in range(u_ref.shape[0])], axis=1)
        state_ref[:, rows] = (base_ref[:, rows] + dot_nt(coefs, bases)).astype(jnp.bfloat16)


def middle_kernel(scales, zero, own, near, next_, far, base, u_ref, v_ref, state_ref, *outs):
    expand(scales, zero, own, near, next_, far, base, u_ref, state_ref)
    project(state_ref[...], v_ref, outs)


def last_kernel(scales, *refs):
    expand(scales, *refs)


def local_kernel(scales, state_ref, leaves_ref, u_ref, v_ref, base_ref):
    dev_rows, leaf = leaves_ref.shape
    levels = u_ref.shape[0]
    coefs = []
    for level in range(levels):
        size = leaf * 2**level
        coefs.append(
            [
                (
                    dot(state_ref[:, pl.ds(start, size)], v_ref[level, pl.ds(start, size), :])
                    * scales[level]
                ).astype(jnp.bfloat16)
                for start in range(0, dev_rows, size)
            ]
        )
    for index, start in enumerate(range(0, dev_rows, leaf)):
        rows = pl.ds(start, leaf)
        left = [state_ref[:, rows]]
        right = [leaves_ref[rows, :]]
        for level in range(levels):
            left.append(coefs[level][(index >> level) ^ 1])
            right.append(u_ref[level, rows, :])
        base_ref[:, rows] = dot_nt(jnp.concatenate(left, axis=1), jnp.concatenate(right, axis=1))


def four_kernel(keep_ref, near_ref, next_ref, far_ref, out_ref):
    out_ref[...] = (keep_ref[...] + near_ref[...]) + (next_ref[...] + far_ref[...])


def line_kernel(arrived_ref, kept_ref, *refs):
    early, (out_ref, *late) = refs[:3], refs[3:]
    out_ref[...] = kept_ref[...] + arrived_ref[...]
    for source, target in zip(early, late):
        target[...] = source[...]


def early_kernel(keep_ref, near_ref, next_ref, far_ref, one_ref, two_ref):
    half, quarter = one_ref.shape[0], two_ref.shape[0]
    skip = near_ref.shape[0] - quarter
    one_ref[...] = next_ref[pl.ds(0, half), :] + far_ref[pl.ds(0, half), :]
    two_ref[...] = (keep_ref[...] + near_ref[pl.ds(skip, quarter), :]) + (
        next_ref[pl.ds(half, quarter), :] + far_ref[pl.ds(half, quarter), :]
    )


def add_kernel(arrived_ref, kept_ref, *refs):
    out_ref = refs[-1]
    rows = out_ref.shape[0]
    out_ref[...] = (
        kept_ref[pl.ds(kept_ref.shape[0] - rows, rows), :]
        + arrived_ref[pl.ds(arrived_ref.shape[0] - rows, rows), :]
    )


def join_kernel(one_ref, *refs):
    *pieces, long_ref, short_ref = refs
    half = one_ref.shape[0]
    rows = pieces[-1].shape[0]
    long_ref[pl.ds(0, half), :] = one_ref[...]
    for i, ref in enumerate(pieces):
        piece = ref[pl.ds(0, rows), :]
        long_ref[pl.ds(half + i * rows, rows), :] = piece
        short_ref[pl.ds(i * rows, rows), :] = piece


def call(kernel, name, outs, *args):
    return pl.pallas_call(
        kernel,
        out_shape=outs,
        in_specs=[VMEM] * len(args),
        out_specs=jax.tree.map(lambda _: VMEM, outs),
        compiler_params=pltpu.CompilerParams(vmem_limit_bytes=6 * 2**20),
        name=name,
    )(*args)


def stack(rows, rank):
    return jax.ShapeDtypeStruct((rows, rank), jnp.float32)


def from_partner(value, axis, mask):
    pairs = [(source, source ^ mask) for source in range(lax.axis_size(axis))]
    return lax.ppermute(value, axis, pairs)


def exchange(parts):
    sends, keep, early, early_keep = parts[:3], parts[3], parts[4:7], parts[7]
    rows, rank = keep.shape
    quarter = early_keep.shape[0]
    half = 2 * quarter
    masks = (1, 2, 3)
    arrived = [from_partner(send, "lo", mask) for send, mask in zip(sends, masks)]
    total = call(four_kernel, "four", stack(rows, rank), keep, *arrived)
    shapes = (stack(rows, rank), *(stack(send.shape[0], rank) for send in early))
    total, *early = call(line_kernel, "line", shapes, from_partner(total, "lo", 6), total, *early)
    early = [from_partner(send, "lo", mask) for send, mask in zip(early, masks)]
    one, two = call(early_kernel, "early", (stack(half, rank), stack(quarter, rank)), early_keep, *early)
    found = [from_partner(two, "lo", 6)]
    for axis, mask in (("lo", 8), ("lo", 24), ("hi", 1), ("hi", 2), ("hi", 6)):
        value = from_partner(total, axis, mask)
        found.append(value)
        rows = total.shape[0] - quarter
        if rows:
            ahead = (two,) if (axis, mask) == ("hi", 1) else ()
            total = call(add_kernel, "add", stack(rows, rank), value, total, *ahead)
    rows = len(found) * quarter
    long, short = call(join_kernel, "join", (stack(half + rows, rank), stack(rows, rank)), one, *found)
    return early[0], long, from_partner(long, "lo", 1), from_partner(short, "lo", 2), from_partner(short, "lo", 3)


def local(vectors, leaves, u_local, v_local, u_upper, v_upper):
    wide, dev_rows = vectors.shape
    leaf = leaves.shape[1]
    rank = u_local.shape[2]
    local_count = u_local.shape[0]
    upper_count = u_upper.shape[0]
    level_count = local_count + upper_count
    scales = [1.0 / math.sqrt(leaf * 2**level * level_count) for level in range(level_count)]
    upper_scales = scales[local_count:]
    half, quarter = wide // 2, wide // 4
    upper = (upper_count - 3) * quarter
    rows = [upper] * 4 + [wide + quarter, half + quarter, half + quarter, quarter]
    part_shapes = tuple(stack(number, rank) for number in rows)
    state_shape = jax.ShapeDtypeStruct((wide, dev_rows), jnp.bfloat16)
    base_shape = jax.ShapeDtypeStruct((wide, dev_rows), jnp.float32)
    state = vectors
    parts = call(first_kernel, "first", part_shapes, state, v_upper)
    for step in range(ITERS):
        found = exchange(parts)
        base = call(
            functools.partial(local_kernel, scales[:local_count]), "local", base_shape, state, leaves, u_local, v_local
        )
        if step < ITERS - 1:
            state, *parts = call(
                functools.partial(middle_kernel, upper_scales), "middle", (state_shape, *part_shapes),
                *found, base, u_upper, v_upper,
            )
        else:
            state = call(functools.partial(last_kernel, upper_scales), "last", state_shape, *found, base, u_upper)
    return state


def solution(mesh):
    return jax.shard_map(
        local,
        mesh=mesh,
        in_specs=(
            P(None, ("hi", "lo")),
            P(("hi", "lo"), None),
            P(None, ("hi", "lo"), None),
            P(None, ("hi", "lo"), None),
            P(None, ("hi", "lo"), None),
            P(None, ("hi", "lo"), None),
        ),
        out_specs=P(None, ("hi", "lo")),
        check_vma=False,
    )
```

```python
import functools
import math

import jax
import jax.numpy as jnp
from jax import lax
from jax.experimental import pallas as pl
from jax.experimental.pallas import tpu as pltpu
from jax.sharding import PartitionSpec as P

ITERS = 4
TILE = 512
NT = (((1,), (1,)), ((), ()))
VMEM = pl.BlockSpec(memory_space=pltpu.VMEM)


def dot(a, b):
    return jnp.dot(a, b, preferred_element_type=jnp.float32)


def dot_nt(a, b):
    return lax.dot_general(a, b, NT, preferred_element_type=jnp.float32)


def sibling(index):
    return index + 1 - 2 * (index % 2)


def place():
    lo = lax.axis_index("lo")
    half = lo % 2
    return half, 2 * half + (lax.div(lo, 2) + lax.div(lo, 4)) % 2


def section(index, rows):
    return pl.ds(pl.multiple_of(index * rows, rows), rows)


def quarters_of(quarter):
    return (quarter + 2) % 4, sibling(quarter), 3 - quarter, quarter


def project(state_ref, v_ref, outs, parts_ref):
    sends, keep_ref, early, early_keep_ref = outs[:3], outs[3], outs[4:7], outs[7]
    own_half, own_quarter = place()
    wide = state_ref.shape[0]
    half, quarter = wide // 2, wide // 4
    levels, _, rank = v_ref.shape

    def two_levels(pair, _):
        level = 2 * pair
        both = dot(state_ref[...], jnp.concatenate([v_ref[level], v_ref[level + 1]], axis=1))
        parts_ref[level] = both[:, :rank]
        parts_ref[level + 1] = both[:, rank:]
        return 0

    lax.fori_loop(0, levels // 2, two_levels, 0)
    early[0][pl.ds(0, wide), :] = parts_ref[0]
    early[1][pl.ds(0, half), :] = parts_ref[1, section(own_half, half), :]
    early[2][pl.ds(0, half), :] = parts_ref[1, section(1 - own_half, half), :]
    targets = ((early[0], wide), (early[1], half), (early[2], half), (early_keep_ref, 0))
    places = quarters_of(own_quarter)
    for (ref, start), index in zip(targets, places):
        ref[pl.ds(start, quarter), :] = parts_ref[2, section(index, quarter), :]
    for level in range(3, levels):
        for ref, index in zip((*sends, keep_ref), places):
            ref[pl.ds((level - 3) * quarter, quarter), :] = parts_ref[level, section(index, quarter), :]


def first_kernel(state_ref, v_ref, *refs):
    *outs, parts_ref = refs
    project(state_ref, v_ref, outs, parts_ref)


def expand(scales, zero_ref, own_ref, near_ref, next_ref, far_ref, base_ref, u_ref, state_ref, coefs_ref):
    wide = base_ref.shape[0]
    half, quarter = wide // 2, wide // 4
    levels, _, rank = u_ref.shape
    own_half, own_quarter = place()

    def put(level, rows, value):
        coefs_ref[rows, pl.ds(level * rank, rank)] = (value * scales[level]).astype(jnp.bfloat16)

    put(0, pl.ds(0, wide), zero_ref[pl.ds(0, wide), :])
    put(1, section(own_half, half), own_ref[pl.ds(0, half), :])
    put(1, section(1 - own_half, half), near_ref[pl.ds(0, half), :])
    for i in range(levels - 2):
        sources = ((near_ref, half), (next_ref, 0), (far_ref, 0), (own_ref, half))
        for (ref, start), index in zip(sources, quarters_of(own_quarter)):
            put(i + 2, section(index, quarter), ref[pl.ds(start + i * quarter, quarter), :])

    def tile(index, _):
        rows = section(index, TILE)
        bases = jnp.concatenate([u_ref[i, rows, :] for i in range(levels)], axis=1)
        state_ref[:, rows] = (base_ref[:, rows] + dot_nt(coefs_ref[...], bases)).astype(jnp.bfloat16)
        return 0

    lax.fori_loop(0, state_ref.shape[1] // TILE, tile, 0)


def middle_kernel(scales, zero, own, near, next_, far, base, u_ref, v_ref, state_ref, *refs):
    *outs, coefs_ref, parts_ref = refs
    expand(scales, zero, own, near, next_, far, base, u_ref, state_ref, coefs_ref)
    project(state_ref, v_ref, outs, parts_ref)


def last_kernel(scales, *refs):
    expand(scales, *refs)


def local_kernel(scales, state_ref, leaves_ref, u_ref, v_ref, base_ref, coefs_ref):
    dev_rows, leaf = leaves_ref.shape
    levels = u_ref.shape[0]
    for level in range(levels):
        size = leaf * 2**level

        def one_node(index, _):
            rows = section(index, size)
            coefs_ref[level, index] = (dot(state_ref[:, rows], v_ref[level, rows, :]) * scales[level]).astype(
                jnp.bfloat16
            )
            return 0

        lax.fori_loop(0, dev_rows // size, one_node, 0)

    def one_leaf(index, _):
        rows = section(index, leaf)
        left = [state_ref[:, rows]]
        right = [leaves_ref[rows, :]]
        for level in range(levels):
            left.append(coefs_ref[level, sibling(lax.div(index, 2**level))])
            right.append(u_ref[level, rows, :])
        base_ref[:, rows] = dot_nt(jnp.concatenate(left, axis=1), jnp.concatenate(right, axis=1))
        return 0

    lax.fori_loop(0, dev_rows // leaf, one_leaf, 0)


def four_kernel(keep_ref, near_ref, next_ref, far_ref, out_ref):
    out_ref[...] = (keep_ref[...] + near_ref[...]) + (next_ref[...] + far_ref[...])


def line_kernel(arrived_ref, kept_ref, *refs):
    early, (out_ref, *late) = refs[:3], refs[3:]
    out_ref[...] = kept_ref[...] + arrived_ref[...]
    for source, target in zip(early, late):
        target[...] = source[...]


def early_kernel(keep_ref, near_ref, next_ref, far_ref, one_ref, two_ref):
    half, quarter = one_ref.shape[0], two_ref.shape[0]
    skip = near_ref.shape[0] - quarter
    one_ref[...] = next_ref[pl.ds(0, half), :] + far_ref[pl.ds(0, half), :]
    two_ref[...] = (keep_ref[...] + near_ref[pl.ds(skip, quarter), :]) + (
        next_ref[pl.ds(half, quarter), :] + far_ref[pl.ds(half, quarter), :]
    )


def add_kernel(arrived_ref, kept_ref, *refs):
    out_ref = refs[-1]
    rows = out_ref.shape[0]
    out_ref[...] = (
        kept_ref[pl.ds(kept_ref.shape[0] - rows, rows), :]
        + arrived_ref[pl.ds(arrived_ref.shape[0] - rows, rows), :]
    )


def join_kernel(one_ref, *refs):
    *pieces, long_ref, short_ref = refs
    half = one_ref.shape[0]
    rows = pieces[-1].shape[0]
    long_ref[pl.ds(0, half), :] = one_ref[...]
    for i, ref in enumerate(pieces):
        piece = ref[pl.ds(0, rows), :]
        long_ref[pl.ds(half + i * rows, rows), :] = piece
        short_ref[pl.ds(i * rows, rows), :] = piece


def call(kernel, name, outs, *args, scratch=()):
    return pl.pallas_call(
        kernel,
        out_shape=outs,
        in_specs=[VMEM] * len(args),
        out_specs=jax.tree.map(lambda _: VMEM, outs),
        scratch_shapes=scratch,
        compiler_params=pltpu.CompilerParams(vmem_limit_bytes=6 * 2**20),
        name=name,
    )(*args)


def stack(rows, rank):
    return jax.ShapeDtypeStruct((rows, rank), jnp.float32)


def from_partner(value, axis, mask):
    pairs = [(source, source ^ mask) for source in range(lax.axis_size(axis))]
    return lax.ppermute(value, axis, pairs)


def exchange(parts):
    sends, keep, early, early_keep = parts[:3], parts[3], parts[4:7], parts[7]
    rows, rank = keep.shape
    quarter = early_keep.shape[0]
    half = 2 * quarter
    masks = (1, 2, 3)
    arrived = [from_partner(send, "lo", mask) for send, mask in zip(sends, masks)]
    total = call(four_kernel, "four", stack(rows, rank), keep, *arrived)
    shapes = (stack(rows, rank), *(stack(send.shape[0], rank) for send in early))
    total, *early = call(line_kernel, "line", shapes, from_partner(total, "lo", 6), total, *early)
    early = [from_partner(send, "lo", mask) for send, mask in zip(early, masks)]
    one, two = call(early_kernel, "early", (stack(half, rank), stack(quarter, rank)), early_keep, *early)
    found = [from_partner(two, "lo", 6)]
    for axis, mask in (("lo", 8), ("lo", 24), ("hi", 1), ("hi", 2), ("hi", 6)):
        value = from_partner(total, axis, mask)
        found.append(value)
        rows = total.shape[0] - quarter
        if rows:
            ahead = (two,) if (axis, mask) == ("hi", 2) else ()
            total = call(add_kernel, "add", stack(rows, rank), value, total, *ahead)
    rows = len(found) * quarter
    long, short = call(join_kernel, "join", (stack(half + rows, rank), stack(rows, rank)), one, *found)
    return early[0], long, from_partner(long, "lo", 1), from_partner(short, "lo", 2), from_partner(short, "lo", 3)


def local(vectors, leaves, u_local, v_local, u_upper, v_upper):
    wide, dev_rows = vectors.shape
    leaf = leaves.shape[1]
    rank = u_local.shape[2]
    local_count = u_local.shape[0]
    upper_count = u_upper.shape[0]
    level_count = local_count + upper_count
    scales = [1.0 / math.sqrt(leaf * 2**level * level_count) for level in range(level_count)]
    upper_scales = scales[local_count:]
    half, quarter = wide // 2, wide // 4
    upper = (upper_count - 3) * quarter
    rows = [upper] * 4 + [wide + quarter, half + quarter, half + quarter, quarter]
    part_shapes = tuple(stack(number, rank) for number in rows)
    state_shape = jax.ShapeDtypeStruct((wide, dev_rows), jnp.bfloat16)
    base_shape = jax.ShapeDtypeStruct((wide, dev_rows), jnp.float32)
    part_scratch = [pltpu.VMEM((upper_count, wide, rank), jnp.float32)]
    coef_scratch = [pltpu.VMEM((wide, upper_count * rank), jnp.bfloat16)]
    local_scratch = [pltpu.VMEM((local_count, dev_rows // leaf, wide, rank), jnp.bfloat16)]
    state = vectors
    parts = call(first_kernel, "first", part_shapes, state, v_upper, scratch=part_scratch)

    def found(state, parts):
        base = call(
            functools.partial(local_kernel, scales[:local_count]), "local", base_shape, state, leaves, u_local, v_local,
            scratch=local_scratch,
        )
        return *exchange(parts), base

    def step(_, carry):
        state, *parts = carry
        return tuple(
            call(
                functools.partial(middle_kernel, upper_scales), "middle", (state_shape, *part_shapes),
                *found(state, parts), u_upper, v_upper, scratch=coef_scratch + part_scratch,
            )
        )

    state, *parts = lax.fori_loop(0, ITERS - 1, step, (state, *parts))
    return call(
        functools.partial(last_kernel, upper_scales), "last", state_shape, *found(state, parts), u_upper,
        scratch=coef_scratch,
    )


def solution(mesh):
    return jax.shard_map(
        local,
        mesh=mesh,
        in_specs=(
            P(None, ("hi", "lo")),
            P(("hi", "lo"), None),
            P(None, ("hi", "lo"), None),
            P(None, ("hi", "lo"), None),
            P(None, ("hi", "lo"), None),
            P(None, ("hi", "lo"), None),
        ),
        out_specs=P(None, ("hi", "lo")),
        check_vma=False,
    )
```

```python
import functools
import math

import jax
import jax.numpy as jnp
from jax import lax
from jax.experimental import pallas as pl
from jax.experimental.pallas import tpu as pltpu
from jax.sharding import PartitionSpec as P

ITERS = 4
TILE = 512
NT = (((1,), (1,)), ((), ()))
VMEM = pl.BlockSpec(memory_space=pltpu.VMEM)


def dot(a, b):
    return jnp.dot(a, b, preferred_element_type=jnp.float32)


def dot_nt(a, b):
    return lax.dot_general(a, b, NT, preferred_element_type=jnp.float32)


def sibling(index):
    return index + 1 - 2 * (index % 2)


def place():
    lo = lax.axis_index("lo")
    half = lo % 2
    return half, 2 * half + (lax.div(lo, 2) + lax.div(lo, 4)) % 2


def section(index, rows):
    return pl.ds(pl.multiple_of(index * rows, rows), rows)


def quarters_of(quarter):
    return (quarter + 2) % 4, sibling(quarter), 3 - quarter, quarter


def project(state_ref, v_ref, outs, parts_ref):
    *sends, keep_ref = outs
    own_half, own_quarter = place()
    wide = state_ref.shape[0]
    half, quarter = wide // 2, wide // 4
    levels, _, rank = v_ref.shape

    def two_levels(pair, _):
        level = 2 * pair
        both = dot(state_ref[...], jnp.concatenate([v_ref[level], v_ref[level + 1]], axis=1))
        parts_ref[level] = both[:, :rank]
        parts_ref[level + 1] = both[:, rank:]
        return 0

    lax.fori_loop(0, levels // 2, two_levels, 0)
    sends[0][pl.ds(0, wide), :] = parts_ref[0]
    sends[1][pl.ds(0, half), :] = parts_ref[1, section(own_half, half), :]
    sends[2][pl.ds(0, half), :] = parts_ref[1, section(1 - own_half, half), :]
    targets = ((sends[0], wide), (sends[1], half), (sends[2], half), (keep_ref, 0))
    for (ref, start), index in zip(targets, quarters_of(own_quarter)):
        for level in range(2, levels):
            rows = pl.ds(start + (level - 2) * quarter, quarter)
            ref[rows, :] = parts_ref[level, section(index, quarter), :]


def first_kernel(state_ref, v_ref, *refs):
    *outs, parts_ref = refs
    project(state_ref, v_ref, outs, parts_ref)


def expand(scales, zero_ref, own_ref, near_ref, next_ref, far_ref, base_ref, u_ref, state_ref, coefs_ref):
    wide = base_ref.shape[0]
    half, quarter = wide // 2, wide // 4
    levels, _, rank = u_ref.shape
    own_half, own_quarter = place()

    def put(level, rows, value):
        coefs_ref[rows, pl.ds(level * rank, rank)] = (value * scales[level]).astype(jnp.bfloat16)

    put(0, pl.ds(0, wide), zero_ref[pl.ds(0, wide), :])
    put(1, section(own_half, half), own_ref[pl.ds(0, half), :])
    put(1, section(1 - own_half, half), near_ref[pl.ds(0, half), :])
    for i in range(levels - 2):
        sources = ((near_ref, half), (next_ref, 0), (far_ref, 0), (own_ref, half))
        for (ref, start), index in zip(sources, quarters_of(own_quarter)):
            put(i + 2, section(index, quarter), ref[pl.ds(start + i * quarter, quarter), :])

    def tile(index, _):
        rows = section(index, TILE)
        bases = jnp.concatenate([u_ref[i, rows, :] for i in range(levels)], axis=1)
        state_ref[:, rows] = (base_ref[:, rows] + dot_nt(coefs_ref[...], bases)).astype(jnp.bfloat16)
        return 0

    lax.fori_loop(0, state_ref.shape[1] // TILE, tile, 0)


def middle_kernel(scales, zero, own, near, next_, far, base, u_ref, v_ref, state_ref, *refs):
    *outs, coefs_ref, parts_ref = refs
    expand(scales, zero, own, near, next_, far, base, u_ref, state_ref, coefs_ref)
    project(state_ref, v_ref, outs, parts_ref)


def last_kernel(scales, *refs):
    expand(scales, *refs)


def local_kernel(scales, state_ref, leaves_ref, u_ref, v_ref, base_ref, coefs_ref):
    dev_rows, leaf = leaves_ref.shape
    levels = u_ref.shape[0]
    for level in range(levels):
        size = leaf * 2**level

        def one_node(index, _):
            rows = section(index, size)
            coefs_ref[level, index] = (dot(state_ref[:, rows], v_ref[level, rows, :]) * scales[level]).astype(
                jnp.bfloat16
            )
            return 0

        lax.fori_loop(0, dev_rows // size, one_node, 0)

    def one_leaf(index, _):
        rows = section(index, leaf)
        left = [state_ref[:, rows]]
        right = [leaves_ref[rows, :]]
        for level in range(levels):
            left.append(coefs_ref[level, sibling(lax.div(index, 2**level))])
            right.append(u_ref[level, rows, :])
        base_ref[:, rows] = dot_nt(jnp.concatenate(left, axis=1), jnp.concatenate(right, axis=1))
        return 0

    lax.fori_loop(0, dev_rows // leaf, one_leaf, 0)


def four_kernel(keep_ref, near_ref, next_ref, far_ref, one_ref, out_ref):
    half, rows = one_ref.shape[0], out_ref.shape[0]
    one_ref[...] = next_ref[pl.ds(0, half), :] + far_ref[pl.ds(0, half), :]
    rest = pl.ds(half, rows)
    out_ref[...] = (keep_ref[...] + near_ref[pl.ds(2 * half, rows), :]) + (next_ref[rest, :] + far_ref[rest, :])


def add_kernel(arrived_ref, kept_ref, out_ref):
    rows = out_ref.shape[0]
    out_ref[...] = (
        kept_ref[pl.ds(kept_ref.shape[0] - rows, rows), :]
        + arrived_ref[pl.ds(arrived_ref.shape[0] - rows, rows), :]
    )


def join_kernel(one_ref, *refs):
    *pieces, long_ref, short_ref = refs
    half = one_ref.shape[0]
    rows = pieces[-1].shape[0]
    long_ref[pl.ds(0, half), :] = one_ref[...]
    for i, ref in enumerate(pieces):
        piece = ref[pl.ds(0, rows), :]
        long_ref[pl.ds(half + i * rows, rows), :] = piece
        short_ref[pl.ds(i * rows, rows), :] = piece


def call(kernel, name, outs, *args, scratch=()):
    return pl.pallas_call(
        kernel,
        out_shape=outs,
        in_specs=[VMEM] * len(args),
        out_specs=jax.tree.map(lambda _: VMEM, outs),
        scratch_shapes=scratch,
        compiler_params=pltpu.CompilerParams(vmem_limit_bytes=6 * 2**20),
        name=name,
    )(*args)


def stack(rows, rank):
    return jax.ShapeDtypeStruct((rows, rank), jnp.float32)


def from_partner(value, axis, mask):
    pairs = [(source, source ^ mask) for source in range(lax.axis_size(axis))]
    return lax.ppermute(value, axis, pairs)


def exchange(parts):
    *sends, keep = parts
    rows, rank = keep.shape
    half = sends[1].shape[0] - rows
    quarter = half // 2
    arrived = [from_partner(send, "lo", mask) for send, mask in zip(sends, (1, 2, 3))]
    one, total = call(four_kernel, "four", (stack(half, rank), stack(rows, rank)), keep, *arrived)
    found = []
    for axis, mask in (("lo", 6), ("lo", 8), ("lo", 24), ("hi", 1), ("hi", 2), ("hi", 6)):
        value = from_partner(total, axis, mask)
        found.append(value)
        left = total.shape[0] - quarter
        if left:
            total = call(add_kernel, "add", stack(left, rank), value, total)
    long, short = call(join_kernel, "join", (stack(half + rows, rank), stack(rows, rank)), one, *found)
    return arrived[0], long, from_partner(long, "lo", 1), from_partner(short, "lo", 2), from_partner(short, "lo", 3)


def local(vectors, leaves, u_local, v_local, u_upper, v_upper):
    wide, dev_rows = vectors.shape
    leaf = leaves.shape[1]
    rank = u_local.shape[2]
    local_count = u_local.shape[0]
    upper_count = u_upper.shape[0]
    level_count = local_count + upper_count
    scales = [1.0 / math.sqrt(leaf * 2**level * level_count) for level in range(level_count)]
    upper_scales = scales[local_count:]
    half, quarter = wide // 2, wide // 4
    upper = (upper_count - 2) * quarter
    rows = [wide + upper, half + upper, half + upper, upper]
    part_shapes = tuple(stack(number, rank) for number in rows)
    state_shape = jax.ShapeDtypeStruct((wide, dev_rows), jnp.bfloat16)
    base_shape = jax.ShapeDtypeStruct((wide, dev_rows), jnp.float32)
    part_scratch = [pltpu.VMEM((upper_count, wide, rank), jnp.float32)]
    coef_scratch = [pltpu.VMEM((wide, upper_count * rank), jnp.bfloat16)]
    local_scratch = [pltpu.VMEM((local_count, dev_rows // leaf, wide, rank), jnp.bfloat16)]
    state = vectors
    parts = call(first_kernel, "first", part_shapes, state, v_upper, scratch=part_scratch)
    for step in range(ITERS):
        found = exchange(parts)
        base = call(
            functools.partial(local_kernel, scales[:local_count]), "local", base_shape, state, leaves, u_local, v_local,
            scratch=local_scratch,
        )
        if step < ITERS - 1:
            state, *parts = call(
                functools.partial(middle_kernel, upper_scales), "middle", (state_shape, *part_shapes),
                *found, base, u_upper, v_upper, scratch=coef_scratch + part_scratch,
            )
        else:
            state = call(
                functools.partial(last_kernel, upper_scales), "last", state_shape, *found, base, u_upper,
                scratch=coef_scratch,
            )
    return state


def solution(mesh):
    return jax.shard_map(
        local,
        mesh=mesh,
        in_specs=(
            P(None, ("hi", "lo")),
            P(("hi", "lo"), None),
            P(None, ("hi", "lo"), None),
            P(None, ("hi", "lo"), None),
            P(None, ("hi", "lo"), None),
            P(None, ("hi", "lo"), None),
        ),
        out_specs=P(None, ("hi", "lo")),
        check_vma=False,
    )
```

```python
import functools
import math

import jax
import jax.numpy as jnp
from jax import lax
from jax.experimental import pallas as pl
from jax.experimental.pallas import tpu as pltpu
from jax.sharding import PartitionSpec as P

ITERS = 4
TILE = 512
NT = (((1,), (1,)), ((), ()))
VMEM = pl.BlockSpec(memory_space=pltpu.VMEM)


def dot(a, b):
    return jnp.dot(a, b, preferred_element_type=jnp.float32)


def dot_nt(a, b):
    return lax.dot_general(a, b, NT, preferred_element_type=jnp.float32)


def sibling(index):
    return index + 1 - 2 * (index % 2)


def place():
    lo = lax.axis_index("lo")
    half = lo % 2
    return half, 2 * half + (lax.div(lo, 2) + lax.div(lo, 4)) % 2


def unrolled(count, step):
    for index in range(count):
        step(index, 0)


def section(index, rows):
    if isinstance(index, int):
        return pl.ds(index * rows, rows)
    return pl.ds(pl.multiple_of(index * rows, rows), rows)


def quarters_of(quarter):
    return (quarter + 2) % 4, sibling(quarter), 3 - quarter, quarter


def project(state_ref, v_ref, outs, parts_ref):
    *sends, keep_ref = outs
    own_half, own_quarter = place()
    wide = state_ref.shape[0]
    half, quarter = wide // 2, wide // 4
    levels, _, rank = v_ref.shape

    def two_levels(pair, _):
        level = 2 * pair
        both = dot(state_ref[...], jnp.concatenate([v_ref[level], v_ref[level + 1]], axis=1))
        parts_ref[level] = both[:, :rank]
        parts_ref[level + 1] = both[:, rank:]
        return 0

    unrolled(levels // 2, two_levels)
    sends[0][pl.ds(0, wide), :] = parts_ref[0]
    sends[1][pl.ds(0, half), :] = parts_ref[1, section(own_half, half), :]
    sends[2][pl.ds(0, half), :] = parts_ref[1, section(1 - own_half, half), :]
    targets = ((sends[0], wide), (sends[1], half), (sends[2], half), (keep_ref, 0))
    for (ref, start), index in zip(targets, quarters_of(own_quarter)):
        for level in range(2, levels):
            rows = pl.ds(start + (level - 2) * quarter, quarter)
            ref[rows, :] = parts_ref[level, section(index, quarter), :]


def first_kernel(state_ref, v_ref, *refs):
    *outs, parts_ref = refs
    project(state_ref, v_ref, outs, parts_ref)


def expand(scales, zero_ref, own_ref, near_ref, next_ref, far_ref, base_ref, u_ref, state_ref, coefs_ref):
    wide = base_ref.shape[0]
    half, quarter = wide // 2, wide // 4
    levels, _, rank = u_ref.shape
    own_half, own_quarter = place()

    def put(level, rows, value):
        coefs_ref[rows, pl.ds(level * rank, rank)] = (value * scales[level]).astype(jnp.bfloat16)

    put(0, pl.ds(0, wide), zero_ref[pl.ds(0, wide), :])
    put(1, section(own_half, half), own_ref[pl.ds(0, half), :])
    put(1, section(1 - own_half, half), near_ref[pl.ds(0, half), :])
    for i in range(levels - 2):
        sources = ((near_ref, half), (next_ref, 0), (far_ref, 0), (own_ref, half))
        for (ref, start), index in zip(sources, quarters_of(own_quarter)):
            put(i + 2, section(index, quarter), ref[pl.ds(start + i * quarter, quarter), :])

    def tile(index, _):
        rows = section(index, TILE)
        bases = jnp.concatenate([u_ref[i, rows, :] for i in range(levels)], axis=1)
        state_ref[:, rows] = (base_ref[:, rows] + dot_nt(coefs_ref[...], bases)).astype(jnp.bfloat16)
        return 0

    unrolled(state_ref.shape[1] // TILE, tile)


def middle_kernel(scales, zero, own, near, next_, far, base, u_ref, v_ref, state_ref, *refs):
    *outs, coefs_ref, parts_ref = refs
    expand(scales, zero, own, near, next_, far, base, u_ref, state_ref, coefs_ref)
    project(state_ref, v_ref, outs, parts_ref)


def last_kernel(scales, *refs):
    expand(scales, *refs)


def local_kernel(scales, state_ref, leaves_ref, u_ref, v_ref, base_ref, coefs_ref):
    dev_rows, leaf = leaves_ref.shape
    levels = u_ref.shape[0]
    for level in range(levels):
        size = leaf * 2**level

        def one_node(index, _):
            rows = section(index, size)
            coefs_ref[level, index] = (dot(state_ref[:, rows], v_ref[level, rows, :]) * scales[level]).astype(
                jnp.bfloat16
            )
            return 0

        unrolled(dev_rows // size, one_node)

    def one_leaf(index, _):
        rows = section(index, leaf)
        left = [state_ref[:, rows]]
        right = [leaves_ref[rows, :]]
        for level in range(levels):
            left.append(coefs_ref[level, sibling(index // 2**level)])
            right.append(u_ref[level, rows, :])
        base_ref[:, rows] = dot_nt(jnp.concatenate(left, axis=1), jnp.concatenate(right, axis=1))
        return 0

    unrolled(dev_rows // leaf, one_leaf)


def four_kernel(keep_ref, near_ref, next_ref, far_ref, one_ref, out_ref):
    half, rows = one_ref.shape[0], out_ref.shape[0]
    one_ref[...] = next_ref[pl.ds(0, half), :] + far_ref[pl.ds(0, half), :]
    rest = pl.ds(half, rows)
    out_ref[...] = (keep_ref[...] + near_ref[pl.ds(2 * half, rows), :]) + (next_ref[rest, :] + far_ref[rest, :])


def add_kernel(arrived_ref, kept_ref, out_ref):
    rows = out_ref.shape[0]
    out_ref[...] = (
        kept_ref[pl.ds(kept_ref.shape[0] - rows, rows), :]
        + arrived_ref[pl.ds(arrived_ref.shape[0] - rows, rows), :]
    )


def join_kernel(one_ref, *refs):
    *pieces, long_ref, short_ref = refs
    half = one_ref.shape[0]
    rows = pieces[-1].shape[0]
    long_ref[pl.ds(0, half), :] = one_ref[...]
    for i, ref in enumerate(pieces):
        piece = ref[pl.ds(0, rows), :]
        long_ref[pl.ds(half + i * rows, rows), :] = piece
        short_ref[pl.ds(i * rows, rows), :] = piece


def call(kernel, name, outs, *args, scratch=()):
    return pl.pallas_call(
        kernel,
        out_shape=outs,
        in_specs=[VMEM] * len(args),
        out_specs=jax.tree.map(lambda _: VMEM, outs),
        scratch_shapes=scratch,
        compiler_params=pltpu.CompilerParams(vmem_limit_bytes=6 * 2**20),
        name=name,
    )(*args)


def stack(rows, rank):
    return jax.ShapeDtypeStruct((rows, rank), jnp.float32)


def from_partner(value, axis, mask):
    pairs = [(source, source ^ mask) for source in range(lax.axis_size(axis))]
    return lax.ppermute(value, axis, pairs)


def exchange(parts):
    *sends, keep = parts
    rows, rank = keep.shape
    half = sends[1].shape[0] - rows
    quarter = half // 2
    arrived = [from_partner(send, "lo", mask) for send, mask in zip(sends, (1, 2, 3))]
    one, total = call(four_kernel, "four", (stack(half, rank), stack(rows, rank)), keep, *arrived)
    found = []
    for axis, mask in (("lo", 6), ("lo", 8), ("lo", 24), ("hi", 1), ("hi", 2), ("hi", 6)):
        value = from_partner(total, axis, mask)
        found.append(value)
        left = total.shape[0] - quarter
        if left:
            total = call(add_kernel, "add", stack(left, rank), value, total)
    long, short = call(join_kernel, "join", (stack(half + rows, rank), stack(rows, rank)), one, *found)
    return arrived[0], long, from_partner(long, "lo", 1), from_partner(short, "lo", 2), from_partner(short, "lo", 3)


def local(vectors, leaves, u_local, v_local, u_upper, v_upper):
    wide, dev_rows = vectors.shape
    leaf = leaves.shape[1]
    rank = u_local.shape[2]
    local_count = u_local.shape[0]
    upper_count = u_upper.shape[0]
    level_count = local_count + upper_count
    scales = [1.0 / math.sqrt(leaf * 2**level * level_count) for level in range(level_count)]
    upper_scales = scales[local_count:]
    half, quarter = wide // 2, wide // 4
    upper = (upper_count - 2) * quarter
    rows = [wide + upper, half + upper, half + upper, upper]
    part_shapes = tuple(stack(number, rank) for number in rows)
    state_shape = jax.ShapeDtypeStruct((wide, dev_rows), jnp.bfloat16)
    base_shape = jax.ShapeDtypeStruct((wide, dev_rows), jnp.float32)
    part_scratch = [pltpu.VMEM((upper_count, wide, rank), jnp.float32)]
    coef_scratch = [pltpu.VMEM((wide, upper_count * rank), jnp.bfloat16)]
    local_scratch = [pltpu.VMEM((local_count, dev_rows // leaf, wide, rank), jnp.bfloat16)]
    state = vectors
    parts = call(first_kernel, "first", part_shapes, state, v_upper, scratch=part_scratch)
    for step in range(ITERS):
        found = exchange(parts)
        base = call(
            functools.partial(local_kernel, scales[:local_count]), "local", base_shape, state, leaves, u_local, v_local,
            scratch=local_scratch,
        )
        if step < ITERS - 1:
            state, *parts = call(
                functools.partial(middle_kernel, upper_scales), "middle", (state_shape, *part_shapes),
                *found, base, u_upper, v_upper, scratch=coef_scratch + part_scratch,
            )
        else:
            state = call(
                functools.partial(last_kernel, upper_scales), "last", state_shape, *found, base, u_upper,
                scratch=coef_scratch,
            )
    return state


def solution(mesh):
    return jax.shard_map(
        local,
        mesh=mesh,
        in_specs=(
            P(None, ("hi", "lo")),
            P(("hi", "lo"), None),
            P(None, ("hi", "lo"), None),
            P(None, ("hi", "lo"), None),
            P(None, ("hi", "lo"), None),
            P(None, ("hi", "lo"), None),
        ),
        out_specs=P(None, ("hi", "lo")),
        check_vma=False,
    )
```
